512 devices in a mesh: img: 32 (over z, y_lo), grp: 2 (over core), flt: 8 (over x, y_hi).
Axes of the slice: x: 4, y: 4 (y_hi: 2, y_lo: 2; y = y_hi * 2 + y_lo), z: 16, core: 2. Of those that a mesh axis runs over, the one named last changes fastest.
Arguments:
- images: bfloat16 [32, 4, 992, 784], P('img', 'grp', 'flt'), may hold values from -6 to 6
- weights: bfloat16 [4, 992, 9, 992], P('grp', 'img', None, 'flt'), may hold values from -0.0625 to 0.0625
Outputs:
- activated: bfloat16 [32, 4, 992, 784], P('img', 'grp', 'flt')
The draws below stay inside these ranges and needn't reach their ends.
All inputs are finite; a program needn't handle non-finite values.
Results may differ from the reference program's by a relative error of at most 0.001.
Values may be sent and summed in bfloat16 or wider, within the bound.
No kernel may reach another device: no remote copies, remote signals or barrier semaphores. Data moves between devices by JAX's collectives and lax.ppermute only.
A program may use at most 64 MiB of HBM per device.

```python
import jax
import jax.numpy as jnp
from jax import lax

GROUPS = 4
CG = 992
SIDE = 28
TAPS = 9
IMAGES = 32
PIXELS = 784


def levels(key, extent, pieces, smallest, high):
    loudness = 1.0
    for position, blocks in pieces:
        steps = jax.random.uniform(jax.random.fold_in(jax.random.fold_in(key, 6), position), (blocks,), jnp.float32, smallest / len(pieces), high / len(pieces))
        loudness = loudness * jnp.repeat(jnp.exp(steps), extent[position] // blocks).reshape((-1,) + (1,) * (len(extent) - 1 - position))
    return loudness


def noise(stream_key, shape, scale, most, cuts=(), kind=jnp.bfloat16):
    entries = jax.random.normal(stream_key, shape, jnp.float32) * scale
    if len(cuts) > 0:
        entries = levels(stream_key, shape, cuts, -0.22, 0.18) * entries
    return jnp.clip(entries, min=-most, max=most).astype(kind)


def setup_inputs(seed: int = 0) -> dict:
    key_of = jax.random.split(jax.random.key(seed), 3)
    return {
        "images": noise(key_of[0], (IMAGES, GROUPS, CG, PIXELS), 1.0, 6.0, ((0, 32), (1, 2), (2, 8))),
        "weights": noise(key_of[1], (GROUPS, CG, TAPS, CG), (TAPS * CG) ** -0.5, 0.0625, ((0, 2), (1, 32), (3, 8))),
    }


def shifted(field, tap):
    row_step = tap // 3 - 1
    col_step = tap % 3 - 1
    pixels = field.shape[-1]
    padded = jnp.pad(field, [(0, 0)] * (field.ndim - 1) + [(SIDE + 1, SIDE + 1)])
    begin = SIDE + 1 + row_step * SIDE + col_step
    moved = lax.slice_in_dim(padded, begin, begin + pixels, axis=field.ndim - 1)
    if col_step != 0:
        column = jnp.arange(pixels) % SIDE
        inside = (column + col_step >= 0) & (column + col_step < SIDE)
        moved = jnp.where(inside, moved, jnp.zeros_like(moved))
    return moved


def reference(images, weights):
    def single(image):
        summed = jnp.zeros((image.shape[0], weights.shape[3], image.shape[2]), jnp.float32)
        for tap in range(TAPS):
            summed = summed + jnp.einsum("gkp,gkm->gmp", shifted(image, tap).astype(jnp.float32), weights[:, :, tap, :].astype(jnp.float32))
        return jnp.maximum(summed, 0.0).astype(jnp.bfloat16)

    return lax.map(single, images)
```

```python
import functools

import jax
import jax.numpy as jnp
from jax import lax
from jax.experimental import pallas as pl
from jax.experimental.pallas import tpu as pltpu
from jax.sharding import PartitionSpec as P


AXES = ("img", "grp", "flt")
SIDE = 28
WIDE = 32
FLAT = SIDE * WIDE
BF16 = jnp.bfloat16


def route(target):
    pairs = []
    for z in range(16):
        for yl in range(2):
            for c in range(2):
                for x in range(4):
                    for yh in range(2):
                        X, YH, YL, Z, C = target(x, yh, yl, z, c)
                        source = ((z * 2 + yl) * 2 + c) * 8 + x * 2 + yh
                        to = (((Z % 16) * 2 + YL) * 2 + C) * 8 + (X % 4) * 2 + YH
                        pairs.append((source, to))
    return pairs


def move(value, target):
    return lax.ppermute(value, AXES, route(target))


def along_y(step):
    def target(x, yh, yl, z, c):
        y = (2 * yh + yl + step) % 4
        return x, y // 2, y % 2, z, c

    return target


def prepare_kernel(info, x_ref, o_ref, wide):
    c = lax.broadcasted_iota(jnp.int32, (124, 128), 0)
    d = lax.broadcasted_iota(jnp.int32, (124, 128), 1)
    skip = (c >= 31).astype(jnp.int32) + (c >= 62).astype(jnp.int32) + (c >= 93).astype(jnp.int32)
    spread = jnp.where(d == c + skip, 1.0, 0.0).astype(BF16)
    keep = lax.broadcasted_iota(jnp.int32, (WIDE, 128), 0) < SIDE
    for t in range(2):
        group = (info[0] + t) % 2
        wide[0:784, :] = jnp.dot(x_ref[group], spread, preferred_element_type=jnp.float32)
        for r in range(SIDE):
            row = wide[SIDE * r : SIDE * r + WIDE, :]
            o_ref[t, WIDE * r : WIDE * r + WIDE, :] = jnp.where(keep, row, 0.0).astype(BF16)


def prepare(images, info):
    return pl.pallas_call(
        prepare_kernel,
        out_shape=jax.ShapeDtypeStruct((2, FLAT, 128), BF16),
        in_specs=[pl.BlockSpec(memory_space=pltpu.SMEM), pl.BlockSpec(memory_space=pltpu.VMEM)],
        out_specs=pl.BlockSpec(memory_space=pltpu.VMEM),
        scratch_shapes=[pltpu.VMEM((800, 128), jnp.float32)],
        name="prepare",
    )(info, images)


def conv_kernel(n_pics, n_filt, info, *refs):
    pics = refs[:n_pics]
    filt = refs[n_pics : n_pics + n_filt]
    o_ref, x_buf, w_buf, acc, rows, sem = refs[n_pics + n_filt :]
    copies = []
    for i, ref in enumerate(filt):
        at = pl.multiple_of(info[1 + i] * 64, 64)
        copies.append(pltpu.make_async_copy(ref, w_buf.at[pl.ds(at, 64), :], sem.at[len(copies)]))
    for i, ref in enumerate(pics):
        for t in range(2):
            block = info[1 + n_filt + 2 * i + t]
            copies.append(pltpu.make_async_copy(ref.at[t], x_buf.at[block], sem.at[len(copies)]))
    for copy in copies:
        copy.start()
    for copy in copies:
        copy.wait()
    for img in range(2):
        slot = (info[0] + img) % 2
        acc[...] = jnp.zeros_like(acc)
        left = jnp.concatenate([x_buf[2 * f + img] for f in range(8)], axis=1)
        for a in range(3):
            product = jnp.dot(left, w_buf[:, 384 * a : 384 * a + 384], preferred_element_type=jnp.float32)
            lo = WIDE * (2 - a)
            for b in range(3):
                acc[b, lo : lo + FLAT, :] += product[:, 128 * b : 128 * b + 128]
        for r in range(SIDE):
            lo = WIDE * (r + 1)
            total = acc[0, lo - 1 : lo - 1 + SIDE, :] + acc[1, lo : lo + SIDE, :]
            total = total + acc[2, lo + 1 : lo + 1 + SIDE, :]
            rows[SIDE * r : SIDE * r + SIDE, :] = jnp.maximum(total, 0.0)
        o_ref[slot] = rows[...].astype(BF16)


def conv(info, pics, filt):
    n_pics, n_filt = len(pics), len(filt)
    hbm = pl.BlockSpec(memory_space=pl.ANY)
    return pl.pallas_call(
        functools.partial(conv_kernel, n_pics, n_filt),
        out_shape=jax.ShapeDtypeStruct((2, 784, 128), BF16),
        in_specs=[pl.BlockSpec(memory_space=pltpu.SMEM)] + [hbm] * (n_pics + n_filt),
        out_specs=pl.BlockSpec(memory_space=pltpu.VMEM),
        scratch_shapes=[
            pltpu.VMEM((16, FLAT, 128), BF16),
            pltpu.VMEM((1024, 1152), BF16),
            pltpu.VMEM((3, 960, 128), jnp.float32),
            pltpu.VMEM((784, 128), jnp.float32),
            pltpu.SemaphoreType.DMA((n_filt + 2 * n_pics,)),
        ],
        name="conv",
    )(info, *pics, *filt)


def shards(images, weights):
    img, core, flt = (lax.axis_index(axis) for axis in AXES)
    z, yl = img // 2, img % 2
    j, plane = z // 2, z % 2
    x, yh = flt // 2, flt % 2
    y = 2 * yh + yl

    packed = jnp.pad(weights, ((0, 0), (0, 1), (0, 0), (0, 4))).reshape(2, 32, 1152)
    packed = jnp.where(yl == 0, packed, packed[::-1])
    piece = {}
    for s in range(2):
        for t in range(2):
            piece[t, s] = move(
                packed[t],
                lambda x, yh, yl, z, c, t=t, s=s: (2 * c + (yl + t) % 2, yh, x // 2, z // 2 * 2 + x % 2, (z + s) % 2),
            )
    chunk = []
    for s in range(2):
        even = jnp.concatenate([piece[0, s], piece[1, s]], axis=0)
        odd = jnp.concatenate([piece[1, s], piece[0, s]], axis=0)
        chunk.append(jnp.where(x % 2 == 0, even, odd))

    ready = prepare(images[0].transpose(0, 2, 1), jnp.stack([x % 2]).astype(jnp.int32))
    halves = []
    for s in range(2):
        got = [
            move(
                ready[t],
                lambda x, yh, yl, z, c, t=t, s=s: (2 * c + (x + t) % 2, yh, yl, z // 2 * 2 + (x // 2 + s) % 2, z % 2),
            )
            for t in range(2)
        ]
        halves.append(jnp.stack(got))

    def ring(x, yh, yl, z, c):
        return x, yh, yl, z + 2 - 4 * c, c

    def other(x, yh, yl, z, c):
        return x, yh, yl, z, 1 - c

    way = 1 - 2 * core
    filt = [chunk[0], chunk[1]]
    place = [2 * j + core, 2 * j + 1 - core]
    held = list(chunk)
    for step in range(1, 5):
        for s in range(2):
            if step == 4 and s == 1:
                continue
            held[s] = move(held[s], ring)
            filt.append(held[s])
            place.append(2 * ((j - step * way) % 8) + (core + s) % 2)
            filt.append(move(held[s], other))
            place.append(2 * ((j + step * way) % 8) + (1 - core + s) % 2)

    pics, source = [], []
    for s in range(2):
        up, down = move(halves[s], along_y(1)), move(halves[s], along_y(-1))
        far = move(up, along_y(1)) if s == 0 else move(down, along_y(-1))
        pics += [halves[s], up, down, far]
        source += [(s, y), (s, (y + 3) % 4), (s, (y + 1) % 4), (s, (y + 2) % 4)]
    blocks = []
    for s, from_y in source:
        for t in range(2):
            from_x = 2 * ((plane + s) % 2) + (x + t) % 2
            blocks.append(2 * (2 * from_x + from_y // 2) + from_y % 2)
    info = jnp.stack([x % 2, *place, *blocks]).astype(jnp.int32)
    out = conv(info, pics, filt)

    back = [
        move(
            out[t],
            lambda x, yh, yl, z, c, t=t: (2 * yl + z % 2, yh, (x + t) % 2, z // 2 * 2 + c, x // 2),
        )
        for t in range(2)
    ]
    both = jnp.where(yl == 0, jnp.stack(back), jnp.stack(back[::-1]))
    return both[:, :, :124].transpose(0, 2, 1)[None]


def solution(mesh):
    in_specs = (P("img", "grp", "flt", None), P("grp", "img", None, "flt"))
    out_specs = P("img", "grp", "flt", None)
    return jax.shard_map(shards, mesh=mesh, in_specs=in_specs, out_specs=out_specs, check_vma=False)
```

```python
import functools

import jax
import jax.numpy as jnp
from jax import lax
from jax.experimental import pallas as pl
from jax.experimental.pallas import tpu as pltpu
from jax.sharding import PartitionSpec as P


AXES = ("img", "grp", "flt")
SIDE = 28
WIDE = 32
FLAT = SIDE * WIDE
BF16 = jnp.bfloat16


def route(target):
    pairs = []
    for z in range(16):
        for yl in range(2):
            for c in range(2):
                for x in range(4):
                    for yh in range(2):
                        X, YH, YL, Z, C = target(x, yh, yl, z, c)
                        source = ((z * 2 + yl) * 2 + c) * 8 + x * 2 + yh
                        to = (((Z % 16) * 2 + YL) * 2 + C) * 8 + (X % 4) * 2 + YH
                        pairs.append((source, to))
    return pairs


def move(value, target):
    return lax.ppermute(value, AXES, route(target))


def along_y(step):
    def target(x, yh, yl, z, c):
        y = (2 * yh + yl + step) % 4
        return x, y // 2, y % 2, z, c

    return target


def prepare_kernel(info, x_ref, first, second, wide):
    c = lax.broadcasted_iota(jnp.int32, (124, 128), 0)
    d = lax.broadcasted_iota(jnp.int32, (124, 128), 1)
    skip = (c >= 31).astype(jnp.int32) + (c >= 62).astype(jnp.int32) + (c >= 93).astype(jnp.int32)
    spread = jnp.where(d == c + skip, 1.0, 0.0).astype(BF16)
    keep = lax.broadcasted_iota(jnp.int32, (WIDE, 128), 0) < SIDE
    for t, o_ref in enumerate((first, second)):
        group = (info[0] + t) % 2
        wide[0:784, :] = jnp.dot(x_ref[group], spread, preferred_element_type=jnp.float32)
        for r in range(SIDE):
            row = wide[SIDE * r : SIDE * r + WIDE, :]
            o_ref[WIDE * r : WIDE * r + WIDE, :] = jnp.where(keep, row, 0.0).astype(BF16)


def prepare(images, info):
    return pl.pallas_call(
        prepare_kernel,
        out_shape=[jax.ShapeDtypeStruct((FLAT, 128), BF16)] * 2,
        in_specs=[pl.BlockSpec(memory_space=pltpu.SMEM), pl.BlockSpec(memory_space=pltpu.VMEM)],
        out_specs=[pl.BlockSpec(memory_space=pltpu.VMEM)] * 2,
        scratch_shapes=[pltpu.VMEM((800, 128), jnp.float32)],
        compiler_params=pltpu.CompilerParams(vmem_limit_bytes=6 << 20),
        name="prepare",
    )(info, images)


def conv_kernel(n_filt, info, *refs):
    filt, pics = refs[:n_filt], refs[n_filt : n_filt + 8]
    first, second, w_buf, acc, rows = refs[n_filt + 8 :]
    at = 2
    for ref in filt:
        for lo in range(0, ref.shape[0], 64):
            w_buf[pl.ds(pl.multiple_of(info[at] * 64, 64), 64), :] = ref[lo : lo + 64, :]
            at += 1
    even = info[1] == 0
    for image in range(2):
        left = []
        for s in range(2):
            half, up, down, far = pics[4 * s : 4 * s + 4]
            for r in range(2):
                for t in range(2):
                    if image == 0:
                        left.append((far if r else half)[t])
                    elif r:
                        left.append(jnp.where(even, up[t], down[t]))
                    else:
                        left.append(jnp.where(even, down[t], up[t]))
        product = jnp.dot(jnp.concatenate(left, axis=1), w_buf[...], preferred_element_type=jnp.float32)
        acc[...] = jnp.zeros_like(acc)
        for tap in range(9):
            lo = WIDE * (2 - tap // 3)
            acc[tap % 3, lo : lo + FLAT, :] += product[:, 128 * tap : 128 * tap + 128]
        for r in range(SIDE):
            lo = WIDE * (r + 1)
            total = acc[0, lo - 1 : lo - 1 + SIDE, :] + acc[1, lo : lo + SIDE, :]
            total = total + acc[2, lo + 1 : lo + 1 + SIDE, :]
            rows[SIDE * r : SIDE * r + SIDE, :] = jnp.maximum(total, 0.0)
        for slot, o_ref in enumerate((first, second)):

            @pl.when(info[0] == (slot + image) % 2)
            def _(o_ref=o_ref):
                o_ref[...] = rows[...].astype(BF16)


def conv(info, pics, filt):
    vmem = pl.BlockSpec(memory_space=pltpu.VMEM)
    return pl.pallas_call(
        functools.partial(conv_kernel, len(filt)),
        out_shape=[jax.ShapeDtypeStruct((784, 128), BF16)] * 2,
        in_specs=[pl.BlockSpec(memory_space=pltpu.SMEM)] + [vmem] * (len(pics) + len(filt)),
        out_specs=[vmem] * 2,
        scratch_shapes=[
            pltpu.VMEM((1024, 1152), BF16),
            pltpu.VMEM((3, 960, 128), jnp.float32),
            pltpu.VMEM((784, 128), jnp.float32),
        ],
        compiler_params=pltpu.CompilerParams(vmem_limit_bytes=24 << 20),
        name="conv",
    )(info, *filt, *pics)


def shards(images, weights):
    img, core, flt = (lax.axis_index(axis) for axis in AXES)
    z, yl = img // 2, img % 2
    j, plane = z // 2, z % 2
    x, yh = flt // 2, flt % 2

    packed = jnp.pad(weights, ((0, 0), (0, 1), (0, 0), (0, 4))).reshape(2, 32, 1152)
    packed = jnp.where(yl == 0, packed, packed[::-1])

    def other(x, yh, yl, z, c):
        return x, yh, yl, z, 1 - c

    piece = [
        move(packed[t], lambda x, yh, yl, z, c, t=t: (2 * c + (yl + t) % 2, yh, x // 2, z // 2 * 2 + x % 2, z % 2))
        for t in range(2)
    ]
    even, odd = (jnp.concatenate(order, axis=0) for order in (piece, piece[::-1]))
    mine = jnp.where(x % 2 == 0, even, odd)
    own = jnp.concatenate([mine, move(mine, other)], axis=0)

    ready = prepare(images[0].transpose(0, 2, 1), jnp.stack([x % 2]).astype(jnp.int32))
    halves = []
    for s in range(2):
        got = [
            move(
                ready[t],
                lambda x, yh, yl, z, c, t=t, s=s: (2 * c + (x + t) % 2, yh, yl, z // 2 * 2 + (x // 2 + s) % 2, z % 2),
            )
            for t in range(2)
        ]
        halves += got

    def ring(x, yh, yl, z, c):
        return x, yh, yl, z + 2 - 4 * c, c

    def places(step, who):
        f = (j + step * (2 * who - 1)) % 8
        s, t, r = (f // 4 + plane) % 2, (f // 2 + x) % 2, (f + yh) % 2
        row = 2 * (4 * s + 2 * r + t)
        return [row + who, row + 1 - who]

    z1 = move(own, ring)
    z2 = move(z1, ring)
    z3 = move(z2, ring)
    z4 = move(z3[:64], ring)
    early = move(jnp.concatenate([z1, z2, z3], axis=0), other)
    late = move(z4, other)
    filt = [own, z1, z2, z3, z4, early, late]
    place = places(0, core) + places(1, core) + places(2, core) + places(3, core) + places(4, core)[:1]
    place += places(1, 1 - core) + places(2, 1 - core) + places(3, 1 - core) + places(4, 1 - core)[:1]

    pics = []
    for s in range(2):
        half = jnp.stack(halves[2 * s : 2 * s + 2])
        up, down = move(half, along_y(1)), move(half, along_y(-1))
        pics += [half, up, down, move(down if s else up, along_y(-1 if s else 1))]
    info = jnp.stack([(yl + x) % 2, yl, *place]).astype(jnp.int32)

    out = conv(info, pics, filt)
    back = [
        move(out[t], lambda x, yh, yl, z, c, t=t: (2 * yl + z % 2, yh, (x + t) % 2, z // 2 * 2 + c, x // 2))
        for t in range(2)
    ]
    both = jnp.where(yl == 0, jnp.stack(back), jnp.stack(back[::-1]))
    return both[:, :, :124].transpose(0, 2, 1)[None]


def solution(mesh):
    in_specs = (P("img", "grp", "flt", None), P("grp", "img", None, "flt"))
    out_specs = P("img", "grp", "flt", None)
    return jax.shard_map(shards, mesh=mesh, in_specs=in_specs, out_specs=out_specs, check_vma=False)
```
